32 devices in a mesh: dp: 8 (over z, y), tensor: 4 (over x, core).
Axes of the slice: x: 2, y: 2, z: 4, core: 2. Of those that a mesh axis runs over, the one named last changes fastest.
Arguments:
- inputs: bfloat16 [608, 8, 1024], P('tensor', 'dp'), may hold values from -6 to 6
- attn_gain: bfloat16 [2, 1024], P(None, 'dp'), may hold values from 0.5 to 1.5
- attn_shift: bfloat16 [2, 1024], P(None, 'dp'), may hold values from -1.25 to 1.25
- qkv_weight: bfloat16 [2, 1024, 3, 1024], P(None, 'dp', None, 'tensor'), may hold values from -0.1875 to 0.1875
- query_bias: bfloat16 [2, 1024], P(None, 'dp'), may hold values from -3 to 3
- value_bias: bfloat16 [2, 1024], P(None, 'dp'), may hold values from -1.25 to 1.25
- out_weight: bfloat16 [2, 1024, 1024], P(None, 'tensor', 'dp'), may hold values from -2 to 2
- out_bias: bfloat16 [2, 1024], P(None, 'dp'), may hold values from -1.25 to 1.25
- mlp_gain: bfloat16 [2, 1024], P(None, 'dp'), may hold values from 0.5 to 1.5
- mlp_shift: bfloat16 [2, 1024], P(None, 'dp'), may hold values from -1.25 to 1.25
- up_weight: bfloat16 [2, 1024, 4096], P(None, 'dp', 'tensor'), may hold values from -0.1875 to 0.1875
- up_bias: bfloat16 [2, 4096], P(None, 'dp'), may hold values from -1.25 to 1.25
- down_weight: bfloat16 [2, 4096, 1024], P(None, 'tensor', 'dp'), may hold values from -0.09375 to 0.09375
- down_bias: bfloat16 [2, 1024], P(None, 'dp'), may hold values from -1.25 to 1.25
- cotangent: bfloat16 [608, 8, 1024], P('tensor', 'dp'), may hold values from -6 to 6
- image_mask: int32 [8], P('dp'), may hold values 0 or 1
- row_mask: int32 [608, 8], P(None, 'dp'), may hold values from 0 to 1, as said below
Outputs:
- outputs: bfloat16 [608, 8, 1024], P('tensor', 'dp')
- grad_inputs: float32 [608, 8, 1024], P('tensor', 'dp')
- grad_attn_gain: float32 [2, 1024], P(None, 'dp')
- grad_attn_shift: float32 [2, 1024], P(None, 'dp')
- grad_qkv_weight: float32 [2, 1024, 3, 1024], P(None, 'dp', None, 'tensor')
- grad_query_bias: float32 [2, 1024], P(None, 'dp')
- grad_value_bias: float32 [2, 1024], P(None, 'dp')
- grad_out_weight: float32 [2, 1024, 1024], P(None, 'tensor', 'dp')
- grad_out_bias: float32 [2, 1024], P(None, 'dp')
- grad_mlp_gain: float32 [2, 1024], P(None, 'dp')
- grad_mlp_shift: float32 [2, 1024], P(None, 'dp')
- grad_up_weight: float32 [2, 1024, 4096], P(None, 'dp', 'tensor')
- grad_up_bias: float32 [2, 4096], P(None, 'dp')
- grad_down_weight: float32 [2, 4096, 1024], P(None, 'tensor', 'dp')
- grad_down_bias: float32 [2, 1024], P(None, 'dp')
The draws below stay inside these ranges and needn't reach their ends.
Inputs may be any that keep to these rules, and one draw needn't show every extreme that they name: `row_mask`: row 0 of every image is live; rows 577 and later are 0.
All inputs are finite; a program needn't handle non-finite values. No bound on the sum of `image_mask` on one device may be relied on, other than what follows from the above.
Results may differ from the reference program's by a relative error of at most 0.015.
Values may be sent and summed in bfloat16 or wider, within the bound.
A program may use at most 128 MiB of HBM per device.

```python
import jax
import jax.numpy as jnp
from jax import lax

D = 1024
HEADS = 16
HEAD_DIM = 64
FF = 4096
TOKENS_IMG = 577
SEQ = 608
LAYERS = 2
IMAGES = 8


def draw_row_mask(key, part):
    position = jnp.arange(SEQ, dtype=jnp.int32)[:, None]
    keep = jax.random.randint(key, (SEQ, IMAGES), 0, 4) > 0
    live = (position < TOKENS_IMG) & ((position == 0) | keep)
    return live.astype(jnp.int32)


def touch_ends(array, rng, low, top_value):
    longest = array.shape.index(max(array.shape))
    spots = []
    for shift in (0, 1):
        where = [jax.random.randint(jax.random.fold_in(rng, axis), (), 0, length) for axis, length in enumerate(array.shape)]
        where[longest] = (where[longest] + shift) % array.shape[longest]
        spots.append(tuple(where))
    return array.at[spots[0]].set(low).at[spots[1]].set(top_value)


def steps_of(own_key, dims, split, low, high):
    loudness = 1.0
    for axis_at, blocks in split:
        heights = jax.random.uniform(jax.random.fold_in(jax.random.fold_in(own_key, 6), axis_at), (blocks,), jnp.float32, low / len(split), high / len(split))
        loudness = loudness * jnp.repeat(jnp.exp(heights), dims[axis_at] // blocks).reshape((-1,) + (1,) * (len(dims) - 1 - axis_at))
    return loudness


def noise(own_key, shape, scale, most, shards=(), held_as=jnp.bfloat16):
    values = jax.random.normal(own_key, shape, jnp.float32) * scale
    if len(shards) > 0:
        values = steps_of(own_key, shape, shards, -0.22, 0.18) * values
    return jnp.clip(values, min=-most, max=most).astype(held_as)


def setup_inputs(seed: int = 0) -> dict:
    splits = jax.random.split(jax.random.key(seed), 18)
    return {
        "inputs": noise(splits[0], (SEQ, IMAGES, D), 1.0, 6.0, ((0, 4), (1, 8))),
        "attn_gain": jnp.clip(1.0 + 0.1 * jax.random.normal(splits[1], (LAYERS, D), jnp.float32), 0.5, 1.5).astype(jnp.bfloat16),
        "attn_shift": noise(splits[2], (LAYERS, D), 0.2, 1.25, ((1, 8),)),
        "qkv_weight": noise(splits[3], (LAYERS, D, 3, D), D ** -0.5, 0.1875, ((1, 8), (3, 4))),
        "query_bias": noise(splits[4], (LAYERS, D), 0.5, 3.0, ((1, 8),)),
        "value_bias": noise(splits[5], (LAYERS, D), 0.2, 1.25, ((1, 8),)),
        "out_weight": noise(splits[6], (LAYERS, D, D), (D // 128) ** -0.5, 2.0, ((1, 4), (2, 8))),
        "out_bias": noise(splits[7], (LAYERS, D), 0.2, 1.25, ((1, 8),)),
        "mlp_gain": jnp.clip(1.0 + 0.1 * jax.random.normal(splits[8], (LAYERS, D), jnp.float32), 0.5, 1.5).astype(jnp.bfloat16),
        "mlp_shift": noise(splits[9], (LAYERS, D), 0.2, 1.25, ((1, 8),)),
        "up_weight": noise(splits[10], (LAYERS, D, FF), D ** -0.5, 0.1875, ((1, 8), (2, 4))),
        "up_bias": noise(splits[11], (LAYERS, FF), 0.2, 1.25, ((1, 8),)),
        "down_weight": noise(splits[12], (LAYERS, FF, D), FF ** -0.5, 0.09375, ((1, 4), (2, 8))),
        "down_bias": noise(splits[13], (LAYERS, D), 0.2, 1.25, ((1, 8),)),
        "cotangent": noise(splits[14], (SEQ, IMAGES, D), 1.0, 6.0, ((0, 4), (1, 8))),
        "image_mask": touch_ends((jax.random.randint(splits[15], (IMAGES,), 0, 4) < 3).astype(jnp.int32), jax.random.fold_in(splits[15], 1), 0, 1),
        "row_mask": draw_row_mask(jax.random.fold_in(splits[17], 71), 0),
    }


@jax.custom_vjp
def low(v):
    return lax.optimization_barrier(v.astype(jnp.bfloat16)).astype(jnp.float32)

@jax.custom_vjp
def low_back(v):
    return v

def low_keep(v):
    return (low(v), None)

def low_pass(kept, grad):
    return (grad,)

def back_keep(v):
    return (v, None)

def back_low(kept, grad):
    return (low(grad),)
low.defvjp(low_keep, low_pass)
low_back.defvjp(back_keep, back_low)

def layer_norm(values, gain, shift):
    center = values - lax.optimization_barrier(jnp.mean(values, -1, keepdims=True))
    inverse = lax.rsqrt(lax.optimization_barrier(jnp.mean(center * center, -1, keepdims=True)) + 1e-05)
    return center * inverse * gain + shift

def quick_gelu(values):
    return values * jax.nn.sigmoid(1.702 * values)

def attend_image(block, live):
    highest = lax.Precision.HIGHEST
    scores = jnp.einsum('qhe,khe->hqk', block[:, 0], block[:, 1], precision=highest) * HEAD_DIM ** (-0.5)
    scores = low_back(scores)
    scores = jnp.where(live[None, None, :] > 0, scores, -1e+30)
    probs = low(jax.nn.softmax(scores, axis=-1))
    return jnp.einsum('hqk,khe->qhe', probs, block[:, 2], precision=highest)

def attend_pair(pair):
    return attend_image(pair[0], pair[1])

def forward(hidden, params, row_mask):
    attn_gain, attn_shift, qkv_weight, query_bias, value_bias, out_weight, out_bias, mlp_gain, mlp_shift, up_weight, up_bias, down_weight, down_bias = params
    highest = lax.Precision.HIGHEST
    live_cols = jnp.transpose(row_mask)
    for depth in range(LAYERS):
        normed = low(layer_norm(hidden, attn_gain[depth], attn_shift[depth]))
        bias_three = jnp.stack([query_bias[depth], jnp.zeros_like(query_bias[depth]), value_bias[depth]])
        qkv = jnp.einsum('sid,dce->sice', normed, qkv_weight[depth], precision=highest) + bias_three
        qkv = low_back(low(qkv))
        blocks = jnp.moveaxis(qkv, 1, 0).reshape(IMAGES, SEQ, 3, HEADS, HEAD_DIM)
        mixed = lax.map(jax.checkpoint(attend_pair), (blocks, live_cols))
        mixed = jnp.moveaxis(mixed.reshape(IMAGES, SEQ, D), 0, 1)
        mixed = low_back(low(mixed))
        branch = low_back(jnp.einsum('sie,ed->sid', mixed, out_weight[depth], precision=highest))
        middle = hidden + branch + out_bias[depth]
        normed_mid = low(layer_norm(middle, mlp_gain[depth], mlp_shift[depth]))
        before = low_back(jnp.einsum('sid,df->sif', normed_mid, up_weight[depth], precision=highest) + up_bias[depth])
        active = low(quick_gelu(before))
        branch_two = low_back(jnp.einsum('sif,fd->sid', active, down_weight[depth], precision=highest))
        hidden = middle + branch_two + down_bias[depth]
    return hidden

def reference(inputs, attn_gain, attn_shift, qkv_weight, query_bias, value_bias, out_weight, out_bias, mlp_gain, mlp_shift, up_weight, up_bias, down_weight, down_bias, cotangent, image_mask, row_mask):
    params = tuple((a.astype(jnp.float32) for a in (attn_gain, attn_shift, qkv_weight, query_bias, value_bias, out_weight, out_bias, mlp_gain, mlp_shift, up_weight, up_bias, down_weight, down_bias)))

    def whole(hidden, *weights):
        return forward(hidden, weights, row_mask)
    result, pull = jax.vjp(whole, inputs.astype(jnp.float32), *params)
    live = (row_mask * image_mask[None, :]).astype(jnp.float32)
    grads = pull(cotangent.astype(jnp.float32) * live[:, :, None])
    return (result.astype(jnp.bfloat16), grads[0], grads[1], grads[2], grads[3], grads[4], grads[5], grads[6], grads[7], grads[8], grads[9], grads[10], grads[11], grads[12], grads[13])
```

```python
import jax
import jax.numpy as jnp
from jax import lax
from jax.sharding import PartitionSpec as P

HEAD_DIM = 64


def layer_norm(values, gain, shift):
    center = values - jnp.mean(values, -1, keepdims=True)
    inverse = lax.rsqrt(jnp.mean(center * center, -1, keepdims=True) + 1e-05)
    return center * inverse * gain + shift


def norm_backward(values, gain, grad_out):
    center = values - jnp.mean(values, -1, keepdims=True)
    inverse = lax.rsqrt(jnp.mean(center * center, -1, keepdims=True) + 1e-05)
    normal = center * inverse
    grad_hat = grad_out * gain
    grad_in = inverse * (
        grad_hat
        - jnp.mean(grad_hat, -1, keepdims=True)
        - normal * jnp.mean(grad_hat * normal, -1, keepdims=True)
    )
    return (grad_in, jnp.sum(grad_out * normal, (0, 1)), jnp.sum(grad_out, (0, 1)))


def quick_gelu(values):
    return values * jax.nn.sigmoid(1.702 * values)


def gelu_slope(values):
    sigma = jax.nn.sigmoid(1.702 * values)
    return sigma + 1.702 * values * sigma * (1.0 - sigma)


def image_scores(block, keep):
    scores = jnp.einsum(
        "qhe,khe->hqk", block[:, 0], block[:, 1], preferred_element_type=jnp.float32
    )
    scores = scores * HEAD_DIM ** (-0.5)
    return jnp.where(keep[None, None, :], scores, -1e30)


def attention_forward(qkv, row_mask):
    seq_len, images, width = (qkv.shape[0], qkv.shape[1], qkv.shape[3])
    heads = width // HEAD_DIM

    def one_image(which, carry):
        outs, lses = carry
        block = lax.dynamic_index_in_dim(qkv, which, 1, keepdims=False).reshape(
            seq_len, 3, heads, HEAD_DIM
        )
        keep = lax.dynamic_index_in_dim(row_mask, which, 1, keepdims=False) > 0
        scores = image_scores(block, keep)
        row_max = jnp.max(scores, -1, keepdims=True)
        expo = jnp.exp(scores - row_max)
        row_total = jnp.sum(expo, -1, keepdims=True)
        weights = (expo / row_total).astype(jnp.bfloat16)
        values = jnp.einsum(
            "hqk,khe->qhe", weights, block[:, 2], preferred_element_type=jnp.float32
        )
        values = values.astype(jnp.bfloat16).reshape(seq_len, 1, width)
        outs = values
        lses = lax.dynamic_update_index_in_dim(
            lses, (row_max + jnp.log(row_total))[:, :, 0], which, 0
        )
        return (outs, lses)

    start = (
        jnp.zeros((seq_len, images, width), jnp.bfloat16),
        jnp.zeros((images, heads, seq_len), jnp.float32),
    )
    return lax.fori_loop(0, images, one_image, start)


def attention_backward(qkv, lses, grad_mixed, row_mask):
    seq_len, images, width = (qkv.shape[0], qkv.shape[1], qkv.shape[3])
    heads = width // HEAD_DIM
    scale = HEAD_DIM ** (-0.5)

    def one_image(which, grads):
        block = lax.dynamic_index_in_dim(qkv, which, 1, keepdims=False).reshape(
            seq_len, 3, heads, HEAD_DIM
        )
        keep = lax.dynamic_index_in_dim(row_mask, which, 1, keepdims=False) > 0
        grad_out = lax.dynamic_index_in_dim(grad_mixed, which, 1, keepdims=False).reshape(
            seq_len, heads, HEAD_DIM
        )
        lse_here = lax.dynamic_index_in_dim(lses, which, 0, keepdims=False)
        weights = jnp.exp(image_scores(block, keep) - lse_here[:, :, None])
        grad_value = jnp.einsum(
            "hqk,qhe->khe",
            weights.astype(jnp.bfloat16),
            grad_out,
            preferred_element_type=jnp.float32,
        )
        grad_weights = jnp.einsum(
            "qhe,khe->hqk", grad_out, block[:, 2], preferred_element_type=jnp.float32
        )
        delta = jnp.sum(weights * grad_weights, -1, keepdims=True)
        grad_scores = (weights * (grad_weights - delta)).astype(jnp.bfloat16)
        grad_query = (
            jnp.einsum("hqk,khe->qhe", grad_scores, block[:, 1], preferred_element_type=jnp.float32)
            * scale
        )
        grad_key = (
            jnp.einsum("hqk,qhe->khe", grad_scores, block[:, 0], preferred_element_type=jnp.float32)
            * scale
        )
        stacked = jnp.stack([grad_query, grad_key, grad_value], 1).astype(jnp.bfloat16)
        return stacked.reshape(seq_len, 1, 3, width)

    return lax.fori_loop(0, images, one_image, jnp.zeros(qkv.shape, jnp.bfloat16))


def body(
    inputs,
    attn_gain,
    attn_shift,
    qkv_weight,
    query_bias,
    value_bias,
    out_weight,
    out_bias,
    mlp_gain,
    mlp_shift,
    up_weight,
    up_bias,
    down_weight,
    down_bias,
    cotangent,
    image_mask,
    row_mask,
):
    depth_count = qkv_weight.shape[0]
    tensor_rank = lax.axis_index("tensor")
    local_rows = inputs.shape[0]
    head_width = qkv_weight.shape[3]
    unit_width = up_weight.shape[2]
    vectors = jnp.stack(
        [attn_gain, attn_shift, query_bias, value_bias, out_bias, mlp_gain, mlp_shift, down_bias], 1
    )

    def fetch(depth):
        return (
            lax.all_gather(qkv_weight[depth], "dp", axis=0, tiled=True),
            lax.all_gather(up_weight[depth], "dp", axis=0, tiled=True),
            lax.all_gather(out_weight[depth], "dp", axis=1, tiled=True),
            lax.all_gather(down_weight[depth], "dp", axis=1, tiled=True),
            lax.all_gather(vectors[depth], "dp", axis=1, tiled=True),
            lax.all_gather(up_bias[depth], "dp", axis=0, tiled=True),
        )

    def unpack(weights):
        vec = weights[4].astype(jnp.float32)
        query_cols = lax.dynamic_slice_in_dim(vec[2], tensor_rank * head_width, head_width)
        value_cols = lax.dynamic_slice_in_dim(vec[3], tensor_rank * head_width, head_width)
        bias_three = jnp.stack([query_cols, jnp.zeros_like(query_cols), value_cols])
        up_cols = lax.dynamic_slice_in_dim(
            weights[5].astype(jnp.float32), tensor_rank * unit_width, unit_width
        )
        return (vec, bias_three, up_cols)

    def forward_parts(hidden, weights):
        qkv_w, up_w, out_w = (weights[0], weights[1], weights[2])
        vec, bias_three, up_cols = unpack(weights)
        normed = layer_norm(hidden, vec[0], vec[1]).astype(jnp.bfloat16)
        product = jnp.einsum(
            "sid,dce->sice",
            lax.all_gather(normed, "tensor", axis=0, tiled=True),
            qkv_w,
            preferred_element_type=jnp.float32,
        )
        qkv = (product + bias_three).astype(jnp.bfloat16)
        mixed, lses = attention_forward(qkv, row_mask)
        middle = (
            hidden
            + lax.psum_scatter(
                jnp.einsum("sie,ed->sid", mixed, out_w, preferred_element_type=jnp.float32).astype(
                    jnp.bfloat16
                ),
                "tensor",
                scatter_dimension=0,
                tiled=True,
            ).astype(jnp.float32)
            + vec[4]
        )
        normed_mid = layer_norm(middle, vec[5], vec[6]).astype(jnp.bfloat16)
        before = (
            jnp.einsum(
                "sid,df->sif",
                lax.all_gather(normed_mid, "tensor", axis=0, tiled=True),
                up_w,
                preferred_element_type=jnp.float32,
            )
            + up_cols
        )
        active = quick_gelu(before).astype(jnp.bfloat16)
        return (normed, qkv, mixed, lses, middle, normed_mid, before, active)

    hidden = inputs.astype(jnp.float32)
    kept = []
    layer_inputs = []
    stored = []
    for depth in range(depth_count):
        weights = fetch(depth)
        kept.append(weights)
        layer_inputs.append(hidden)
        parts = forward_parts(hidden, weights)
        stored.append(parts)
        down_cols = weights[4][7].astype(jnp.float32)
        mlp_active = parts[7]
        mlp_down_w = weights[3]
        hidden = (
            parts[4]
            + lax.psum_scatter(
                jnp.einsum(
                    "sif,fd->sid", mlp_active, mlp_down_w, preferred_element_type=jnp.float32
                ).astype(jnp.bfloat16),
                "tensor",
                scatter_dimension=0,
                tiled=True,
            ).astype(jnp.float32)
            + down_cols
        )
    live_rows = lax.dynamic_slice_in_dim(row_mask, tensor_rank * local_rows, local_rows, 0)
    live = (live_rows * image_mask[None, :]).astype(jnp.float32)
    grad = cotangent.astype(jnp.float32) * live[:, :, None]
    per_layer = []
    for depth in reversed(range(depth_count)):
        weights = kept[depth]
        parts = stored[depth]
        layer_qkv_w = weights[0]
        layer_up_w = weights[1]
        layer_out_w = weights[2]
        down_w = weights[3]
        layer_vec, layer_bias_three, layer_up_cols = unpack(weights)
        (
            layer_normed,
            layer_qkv,
            layer_mixed,
            layer_lses,
            layer_middle,
            layer_normed_mid,
            layer_before,
            layer_active,
        ) = parts
        full_width = layer_vec.shape[1]
        grad_down_bias = jnp.sum(grad, (0, 1))
        fold_piece = lax.all_gather(grad.astype(jnp.bfloat16), "tensor", axis=0, tiled=True)
        update = jnp.einsum("sid,fd->sif", fold_piece, down_w, preferred_element_type=jnp.float32)
        grad_down_w = jnp.einsum(
            "sif,sid->df", layer_active, fold_piece, preferred_element_type=jnp.float32
        )
        grad_before = (update * gelu_slope(layer_before)).astype(jnp.bfloat16)
        grad_up_cols = jnp.sum(grad_before.astype(jnp.float32), (0, 1))
        grad_up_w = jnp.einsum(
            "sid,sif->df",
            lax.all_gather(layer_normed_mid, "tensor", axis=0, tiled=True),
            grad_before,
            preferred_element_type=jnp.float32,
        )
        grad_normed_mid = lax.psum_scatter(
            jnp.einsum(
                "sif,df->sid", grad_before, layer_up_w, preferred_element_type=jnp.float32
            ).astype(jnp.bfloat16),
            "tensor",
            scatter_dimension=0,
            tiled=True,
        ).astype(jnp.float32)
        grad_mid, grad_mlp_gain, grad_mlp_shift = norm_backward(
            layer_middle, layer_vec[5], grad_normed_mid
        )
        grad_mid = grad_mid + grad
        grad_out_bias = jnp.sum(grad_mid, (0, 1))
        piece = lax.all_gather(grad_mid.astype(jnp.bfloat16), "tensor", axis=0, tiled=True)
        fold_update = jnp.einsum(
            "sid,ed->sie", piece, layer_out_w, preferred_element_type=jnp.float32
        )
        grad_out_w = jnp.einsum(
            "sie,sid->de", layer_mixed, piece, preferred_element_type=jnp.float32
        )
        grad_qkv = attention_backward(
            layer_qkv, layer_lses, fold_update.astype(jnp.bfloat16), row_mask
        )
        grad_bias_three = jnp.sum(grad_qkv.astype(jnp.float32), (0, 1))
        grad_qkv_w = jnp.einsum(
            "sid,sice->dce",
            lax.all_gather(layer_normed, "tensor", axis=0, tiled=True),
            grad_qkv,
            preferred_element_type=jnp.float32,
        )
        grad_normed = lax.psum_scatter(
            jnp.einsum(
                "sice,dce->sid", grad_qkv, layer_qkv_w, preferred_element_type=jnp.float32
            ).astype(jnp.bfloat16),
            "tensor",
            scatter_dimension=0,
            tiled=True,
        ).astype(jnp.float32)
        grad_in, grad_attn_gain, grad_attn_shift = norm_backward(
            layer_inputs[depth], layer_vec[0], grad_normed
        )
        grad_in = grad_in + grad_mid
        empty = jnp.zeros((full_width,), jnp.float32)
        grad_query = lax.dynamic_update_slice_in_dim(
            empty, grad_bias_three[0], tensor_rank * head_width, 0
        )
        grad_value = lax.dynamic_update_slice_in_dim(
            empty, grad_bias_three[2], tensor_rank * head_width, 0
        )
        grad_up_full = lax.dynamic_update_slice_in_dim(
            jnp.zeros((weights[5].shape[0],), jnp.float32),
            grad_up_cols,
            tensor_rank * unit_width,
            0,
        )
        grad_vec = jnp.stack(
            [
                grad_attn_gain,
                grad_attn_shift,
                grad_query,
                grad_value,
                grad_out_bias,
                grad_mlp_gain,
                grad_mlp_shift,
                grad_down_bias,
            ]
        )
        flat = jnp.concatenate(
            [
                grad_qkv_w.reshape(grad_qkv_w.shape[0], -1),
                grad_up_w,
                grad_out_w,
                grad_down_w,
            ],
            1,
        ).astype(jnp.bfloat16)
        flat = lax.psum_scatter(flat, "dp", scatter_dimension=0, tiled=True).astype(jnp.float32)
        ends = [3 * head_width, 3 * head_width + unit_width, 4 * head_width + unit_width]
        part_qkv, part_up, part_out, part_down = jnp.split(flat, ends, 1)
        shards = (
            part_qkv.reshape(-1, 3, head_width),
            part_up,
            part_out.T,
            part_down.T,
            grad_vec,
            grad_up_full,
        )
        grad = grad_in
        per_layer.insert(0, shards)
    vec_grads = jnp.stack([shards[4] for shards in per_layer])
    bias_grads = jnp.stack([shards[5] for shards in per_layer])
    whole_vec = jnp.concatenate([vec_grads, bias_grads.reshape(depth_count, -1, full_width)], 1)
    whole_vec = lax.psum(whole_vec, ("dp", "tensor"))
    dp_rank = lax.axis_index("dp")
    shard_width = attn_gain.shape[1]
    vec_sum = lax.dynamic_slice_in_dim(
        whole_vec[:, :8], dp_rank * shard_width, shard_width, 2
    )
    up_sum = lax.dynamic_slice_in_dim(
        whole_vec[:, 8:].reshape(depth_count, -1), dp_rank * up_bias.shape[1], up_bias.shape[1], 1
    )
    return (
        hidden.astype(jnp.bfloat16),
        grad,
        vec_sum[:, 0],
        vec_sum[:, 1],
        jnp.stack([shards[0] for shards in per_layer]),
        vec_sum[:, 2],
        vec_sum[:, 3],
        jnp.stack([shards[2] for shards in per_layer]),
        vec_sum[:, 4],
        vec_sum[:, 5],
        vec_sum[:, 6],
        jnp.stack([shards[1] for shards in per_layer]),
        up_sum,
        jnp.stack([shards[3] for shards in per_layer]),
        vec_sum[:, 7],
    )


def solution(mesh):
    in_specs = (
        P("tensor", "dp", None),
        P(None, "dp"),
        P(None, "dp"),
        P(None, "dp", None, "tensor"),
        P(None, "dp"),
        P(None, "dp"),
        P(None, "tensor", "dp"),
        P(None, "dp"),
        P(None, "dp"),
        P(None, "dp"),
        P(None, "dp", "tensor"),
        P(None, "dp"),
        P(None, "tensor", "dp"),
        P(None, "dp"),
        P("tensor", "dp", None),
        P("dp"),
        P(None, "dp"),
    )
    out_specs = (
        P("tensor", "dp", None),
        P("tensor", "dp", None),
        P(None, "dp"),
        P(None, "dp"),
        P(None, "dp", None, "tensor"),
        P(None, "dp"),
        P(None, "dp"),
        P(None, "tensor", "dp"),
        P(None, "dp"),
        P(None, "dp"),
        P(None, "dp"),
        P(None, "dp", "tensor"),
        P(None, "dp"),
        P(None, "tensor", "dp"),
        P(None, "dp"),
    )
    return jax.shard_map(body, mesh=mesh, in_specs=in_specs, out_specs=out_specs, check_vma=False)
```
